1024 devices in a mesh: grp: 16 (over y, core), shard: 16 (over z), side: 4 (over x).
Axes of the slice: x: 4, y: 8, z: 16, core: 2. Of those that a mesh axis runs over, the one named last changes fastest.
Arguments:
- tokens: bfloat16 [4096, 4096], P(('grp', 'side')), may hold values from -6 to 6
- routes: int32 [4096, 8], P(('grp', 'side')), may hold values from 0 to 63, all different within a row; in each aligned block of 64 rows (0 to 63, 64 to 127, ...) at most 16 rows name the same one
- probs: float32 [4096, 8], P(('grp', 'side')), may hold values from 0.02 to 1
- w_gate: bfloat16 [256, 4096, 256], P(('grp', 'shard')), may hold values from -0.09375 to 0.09375
- w_up: bfloat16 [256, 4096, 256], P(('grp', 'shard')), may hold values from -0.09375 to 0.09375
- w_down: bfloat16 [256, 256, 4096], P(('grp', 'shard')), may hold values from -0.1875 to 0.1875
Outputs:
- mixed: bfloat16 [4096, 4096], P(('grp', 'side'), 'shard')
The draws below stay inside these ranges and needn't reach their ends.
Inputs may be any that keep to these rules, and one draw needn't show every extreme that they name: `routes`: each token names 8 different experts. Within each aligned block of 64 tokens no expert is named by more than 16 tokens, a bound that some block reaches.
All inputs are finite; a program needn't handle non-finite values.
Results may differ from the reference program's by a relative error of at most 0.0057.
Values may be sent and summed in bfloat16 or wider, within the bound.
No kernel may reach another device: no remote copies, remote signals or barrier semaphores. Data moves between devices by JAX's collectives and lax.ppermute only.
A program may use at most 32 MiB of HBM per device.

```python
import math
import jax
import jax.numpy as jnp
import numpy as np
from jax import lax

D = 4096
FF = 1024
TPE = 4
TILE_FF = 256
EXPERTS = 64
TOP = 8
TOK_GS = 64
CAP = 16
TOKENS = 4096
ROWMAX = 1024


def block_levels(key, extent, cuts, low, largest):
    gain = 1.0
    for dim, blocks in cuts:
        heights = jax.random.uniform(jax.random.fold_in(jax.random.fold_in(key, 6), dim), (blocks,), jnp.float32, low / len(cuts), largest / len(cuts))
        gain = gain * jnp.repeat(jnp.exp(heights), extent[dim] // blocks).reshape((-1,) + (1,) * (len(extent) - 1 - dim))
    return gain


def shared_out(key, own, number, rows, count, top, most, slope):
    sequence = jax.random.permutation(key, count)
    crowded, ordinary = portions_of(count, rows * top, most, slope, True), portions_of(count, rows * top, most, slope, False)
    places = jnp.arange(count)

    def named(sizes, rotation):
        used = int((sizes > 0).sum())
        fixed = max(1, used // 4)
        moved = fixed + (places - fixed + rotation * (used - fixed)) % max(1, count - fixed)
        return jnp.zeros((count,), jnp.int32).at[sequence[jnp.where(places < fixed, places, moved)]].set(jnp.asarray(sizes, jnp.int32))

    sizes = jnp.where(number % 4 == 0, named(crowded, number // 4), named(ordinary, number - number // 4 - 1))
    mixed = jax.random.permutation(jax.random.fold_in(own, 3), count)
    donor, sink = mixed[0:count // 2 * 2:2], mixed[1:count // 2 * 2:2]
    slack = jnp.minimum(sizes[donor] - 1, most - sizes[sink]) // 2
    slack = jnp.where((donor == sequence[0]) | (sink == sequence[0]) | (sizes[sink] == 0), 0, jnp.maximum(slack, 0))
    moved = jax.random.randint(jax.random.fold_in(own, 4), (count // 2,), 0, 1 << 20) % (slack + 1)
    sizes = sizes.at[donor].add(-moved).at[sink].add(moved)
    labels = jnp.searchsorted(jnp.cumsum(sizes), jnp.arange(rows * top), side="right").astype(jnp.int32)
    table = labels.reshape(top, rows).T
    table = table[jax.random.permutation(jax.random.fold_in(own, 1), rows)]
    rotation = jax.random.randint(jax.random.fold_in(own, 2), (rows, 1), 0, top)
    return jnp.take_along_axis(table, (jnp.arange(top)[None, :] + rotation) % top, axis=1)


def portions_of(number_of, total, limit, lean, full):
    weights = [(1 << 20) // math.isqrt(grade ** lean) + 1 for grade in range(1, number_of + 1)]
    largest = limit if full else min(limit, max(-(-total // number_of), total * weights[0] // sum(weights)))
    least = 1 if total - largest >= number_of - 1 else 0
    given, surplus = [largest] + [least] * (number_of - 1), total - largest - least * (number_of - 1)
    while surplus > 0:
        free = [i for i in range(1, number_of) if given[i] < largest] or [i for i in range(1, number_of) if given[i] < limit]
        whole, budget = sum([weights[i] for i in free]), surplus
        for i in free:
            more = min(limit - given[i], max(1, budget * weights[i] // whole), surplus)
            given[i] = given[i] + more
            surplus = surplus - more
    return np.array(given)


def noise(own_key, extent, scale, most, split=(), held_as=jnp.bfloat16):
    values = scale * jax.random.normal(own_key, extent, jnp.float32)
    if split:
        values = values * block_levels(own_key, extent, split, -0.22, 0.18)
    return jnp.clip(values, -most, most).astype(held_as)


def setup_inputs(seed: int = 0) -> dict:
    splits = jax.random.split(jax.random.key(seed), 7)
    tokens = noise(splits[0], (TOKENS, D), 1.0, 6.0, ((0, 64),))
    routes_keys = jax.random.split(jax.random.fold_in(splits[1], 1), TOKENS // TOK_GS)
    routes_turns = jax.random.permutation(jax.random.fold_in(splits[1], 3), TOKENS // TOK_GS)
    routes = jax.vmap(lambda own, number: shared_out(jax.random.fold_in(splits[1], 2), own, number, TOK_GS, EXPERTS, TOP, CAP, 2))(routes_keys, routes_turns).reshape((TOKENS, TOP))
    probs = jnp.clip(jnp.exp(math.log(1.0) - 3.912023 * jax.random.uniform(splits[2], (TOKENS, TOP), jnp.float32) ** block_levels(splits[2], (TOKENS, TOP), ((0, 64),), -0.2, 0.2)), 0.02, 1.0)
    w_gate = noise(splits[3], (EXPERTS * TPE, D, TILE_FF), D ** -0.5, 0.09375, ((0, 256),))
    w_up = noise(splits[4], (EXPERTS * TPE, D, TILE_FF), D ** -0.5, 0.09375, ((0, 256),))
    w_down = noise(splits[5], (EXPERTS * TPE, TILE_FF, D), FF ** -0.5, 0.1875, ((0, 256),))
    return {"tokens": tokens, "routes": routes, "probs": probs, "w_gate": w_gate, "w_up": w_up, "w_down": w_down}


def reference(tokens, routes, probs, w_gate, w_up, w_down):
    gates = probs / jnp.sum(probs, axis=-1, keepdims=True)
    gate_tiles = w_gate.reshape(EXPERTS, TPE, D, TILE_FF)
    up_tiles = w_up.reshape(EXPERTS, TPE, D, TILE_FF)
    down_tiles = w_down.reshape(EXPERTS, TPE, TILE_FF, D)
    positions = jnp.arange(ROWMAX)

    def one_expert(expert, total):
        match = routes == expert
        chosen = jnp.any(match, axis=1)
        weight = jnp.sum(jnp.where(match, gates, jnp.float32(0.0)), axis=1)
        index = jnp.nonzero(chosen, size=ROWMAX, fill_value=0)[0].astype(jnp.int32)
        valid = positions < jnp.sum(chosen.astype(jnp.int32))
        rows = tokens[index]
        summed = jnp.zeros((ROWMAX, D), jnp.float32)
        for tile in range(TPE):
            gate = jnp.dot(rows, gate_tiles[expert, tile], preferred_element_type=jnp.float32)
            upper = jnp.dot(rows, up_tiles[expert, tile], preferred_element_type=jnp.float32)
            hidden = (jax.nn.silu(gate) * upper).astype(jnp.bfloat16)
            part = jnp.dot(hidden, down_tiles[expert, tile], preferred_element_type=jnp.float32).astype(jnp.bfloat16)
            summed = summed + part.astype(jnp.float32)
        scale = jnp.where(valid, weight[index], jnp.float32(0.0))
        return total.at[index].add(summed * scale[:, None])

    total = lax.fori_loop(0, EXPERTS, one_expert, jnp.zeros((TOKENS, D), jnp.float32))
    return total.astype(jnp.bfloat16)
```

```python
import jax
import jax.numpy as jnp
from jax import lax
from jax.sharding import PartitionSpec as P

TPE = 4


def tile_pass(rows, w_gate, w_up, w_down):
    gate = jnp.dot(rows, w_gate[0], preferred_element_type=jnp.float32)
    upper = jnp.dot(rows, w_up[0], preferred_element_type=jnp.float32)
    hidden = (jax.nn.silu(gate) * upper).astype(jnp.bfloat16)
    return jnp.dot(hidden, w_down[0], preferred_element_type=jnp.float32).astype(jnp.bfloat16)


def on_device(tokens, routes, probs, w_gate, w_up, w_down):
    groups = lax.axis_size("grp")
    shards = lax.axis_size("shard")
    per_group = shards // TPE
    experts_all = groups * per_group
    tok_count, width = tokens.shape
    top_count = routes.shape[1]
    capacity = 2 * tok_count * top_count // experts_all
    local = lax.axis_index("shard") // TPE
    targets = jnp.arange(groups, dtype=jnp.int32) * per_group + local
    gates = probs / jnp.sum(probs, axis=-1, keepdims=True)
    match = routes[:, :, None] == targets[None, None, :]
    hits = jnp.any(match, axis=1)
    gate_hits = jnp.sum(jnp.where(match, gates[:, :, None], jnp.float32(0.0)), axis=1)
    before = jnp.tril(jnp.ones((tok_count, tok_count), jnp.bfloat16), -1)
    ranks = jnp.dot(before, hits.astype(jnp.bfloat16), preferred_element_type=jnp.float32)
    slots = jnp.arange(capacity, dtype=jnp.int32)
    ranks = ranks.astype(jnp.int32)
    chosen = hits[:, :, None] & (ranks[:, :, None] == slots[None, None, :])
    select = chosen.astype(jnp.bfloat16).reshape(tok_count, groups * capacity)
    weight = jnp.where(chosen, gate_hits[:, :, None], jnp.float32(0.0))
    weight = weight.reshape(tok_count, groups * capacity)
    high = weight.astype(jnp.bfloat16)
    low = (weight - high.astype(jnp.float32)).astype(jnp.bfloat16)
    outgoing = lax.dot_general(
        select, tokens, (((0,), (0,)), ((), ())), preferred_element_type=jnp.float32
    ).astype(jnp.bfloat16)
    arrived = lax.all_to_all(outgoing, "grp", split_axis=0, concat_axis=0, tiled=True)
    results = tile_pass(arrived, w_gate, w_up, w_down)
    returned = lax.all_to_all(results, "grp", split_axis=0, concat_axis=0, tiled=True)
    both = jnp.concatenate([high, low], axis=0)
    mixed = jnp.dot(both, returned, preferred_element_type=jnp.float32)
    combined = (mixed[:tok_count] + mixed[tok_count:]).astype(jnp.bfloat16)
    pieces = combined.reshape(tok_count, shards, width // shards).transpose(1, 0, 2)
    pieces = lax.all_to_all(pieces, "shard", split_axis=0, concat_axis=0, tiled=True)
    return jnp.sum(pieces.astype(jnp.float32), axis=0).astype(jnp.bfloat16)


def solution(mesh):
    return jax.shard_map(
        on_device,
        mesh=mesh,
        in_specs=(
            P(("grp", "side"), None),
            P(("grp", "side"), None),
            P(("grp", "side"), None),
            P(("grp", "shard"), None, None),
            P(("grp", "shard"), None, None),
            P(("grp", "shard"), None, None),
        ),
        out_specs=P(("grp", "side"), "shard"),
        check_vma=False,
    )
```

```python
import functools

import jax
import jax.numpy as jnp
from jax import lax
from jax.experimental import pallas as pl
from jax.experimental.pallas import tpu as pltpu
from jax.sharding import PartitionSpec as P


TPE = 4
BF16 = jnp.bfloat16
F32 = jnp.float32


def dot(a, b, dims=((1,), (0,))):
    return lax.dot_general(a, b, (dims, ((), ())), preferred_element_type=F32)


def dispatch_kernel(cap, per_group, place, routes, probs, tokens, sent, high, low):
    rows, tok = high.shape
    row = lax.broadcasted_iota(jnp.int32, (rows, tok), 0)
    target = lax.shift_right_logical(row, cap.bit_length() - 1) * per_group + place[0]
    slot = lax.bitwise_and(row, cap - 1).astype(F32)
    gates = probs[...] / jnp.sum(probs[...], axis=0, keepdims=True)
    hits = jnp.zeros((rows, tok), F32)
    weight = jnp.zeros((rows, tok), F32)
    for k in range(routes.shape[0]):
        match = routes[k : k + 1, :] == target
        hits = jnp.where(match, F32(1.0), hits)
        weight = jnp.where(match, gates[k : k + 1, :], weight)
    before = lax.broadcasted_iota(jnp.int32, (tok, tok), 0)
    before = before < lax.broadcasted_iota(jnp.int32, (tok, tok), 1)
    ranks = dot(hits.astype(BF16), jnp.where(before, F32(1.0), F32(0.0)).astype(BF16))
    chosen = (hits > 0.5) & (ranks == slot)
    select = jnp.where(chosen, F32(1.0), F32(0.0)).astype(BF16)
    weight = jnp.where(chosen, weight, F32(0.0))
    top = weight.astype(BF16)
    high[...] = top
    low[...] = (weight - top.astype(F32)).astype(BF16)
    step = min(512, sent.shape[1])
    for at in range(0, sent.shape[1], step):
        sent[:, at : at + step] = dot(select, tokens[:, at : at + step]).astype(BF16)


def shuffle_kernel(block, place, weights, *outs):
    for k, out in enumerate(outs):
        owner = lax.bitwise_xor(place[1], k)
        for m in range(out.shape[1] // block):
            at = pl.multiple_of((m * TPE + owner) * block, block)
            out[:, m * block : (m + 1) * block] = weights[:, pl.ds(at, block)]


def hidden_kernel(rows, w_gate, w_up, out):
    gate = dot(rows[...], w_gate[...])
    upper = dot(rows[...], w_up[...])
    out[...] = (gate / (1.0 + jnp.exp(-gate)) * upper).astype(BF16)


def down_kernel(*refs):
    hidden, weights, out = refs[:TPE], refs[TPE : 2 * TPE], refs[-1]
    step = min(256, out.shape[1])
    for at in range(0, out.shape[1], step):
        total = dot(hidden[0][...], weights[0][:, at : at + step])
        for k in range(1, TPE):
            total = total + dot(hidden[k][...], weights[k][:, at : at + step])
        out[:, at : at + step] = total.astype(BF16)


def combine_kernel(place, high, low, rows, kept, *sent):
    block = kept.shape[1]
    for k in range(TPE):
        at = pl.multiple_of(lax.bitwise_xor(place[0], k) * block, block)
        piece = rows[:, pl.ds(at, block)]
        total = dot(high[...], piece, ((0,), (0,))) + dot(low[...], piece, ((0,), (0,)))
        if k == 0:
            kept[...] = total
        else:
            sent[k - 1][...] = total.astype(BF16)


def finish_kernel(kept, *refs):
    total = kept[...]
    for part in refs[:-1]:
        total = total + part[...].astype(F32)
    refs[-1][...] = total.astype(BF16)


def call(kernel, shapes, *args, flops=0):
    specs = [pl.BlockSpec(memory_space=pltpu.VMEM)] * len(args)
    if args[0].ndim == 1:
        specs[0] = pl.BlockSpec(memory_space=pltpu.SMEM)
    outs = [jax.ShapeDtypeStruct(s, d) for s, d in shapes]
    moved = sum(a.size * a.dtype.itemsize for a in (*args, *outs))
    return pl.pallas_call(
        kernel,
        out_shape=outs,
        in_specs=specs,
        out_specs=[pl.BlockSpec(memory_space=pltpu.VMEM)] * len(outs),
        compiler_params=pltpu.CompilerParams(vmem_limit_bytes=16 << 20),
        cost_estimate=pl.CostEstimate(flops=flops, bytes_accessed=moved, transcendentals=0),
    )(*args)


def on_device(tokens, routes, probs, w_gate, w_up, w_down):
    groups, shards = lax.axis_size("grp"), lax.axis_size("shard")
    per_group = shards // TPE
    tok, width = tokens.shape
    units = w_down.shape[1]
    block, quarter = width // shards, width // TPE
    cap = 2 * tok * routes.shape[1] // (groups * per_group)
    rows = groups * cap
    z = lax.axis_index("shard")
    place = jnp.stack([z // TPE, lax.rem(z, TPE)]).astype(jnp.int32)

    def over_y(x):
        x = lax.all_to_all(x.reshape(groups, cap, -1), "grp", 0, 0, tiled=True)
        return x.reshape(rows, -1)

    def swap(x, bits):
        return lax.ppermute(x, "shard", [(i, i ^ bits) for i in range(shards)])

    sent, high, low = call(
        functools.partial(dispatch_kernel, cap, per_group),
        [((rows, width), BF16), ((rows, tok), BF16), ((rows, tok), BF16)],
        place, routes.T, probs.T, tokens, flops=2 * rows * tok * width,
    )
    arrived = over_y(sent)
    parts = call(
        functools.partial(shuffle_kernel, block),
        [((units, quarter), BF16)] * TPE, place, w_down[0],
    )
    weights = [parts[0]] + [swap(parts[k], k) for k in range(1, TPE)]
    (hidden,) = call(
        hidden_kernel, [((rows, units), BF16)], arrived, w_gate[0], w_up[0],
        flops=4 * rows * width * units,
    )
    hiddens = [hidden] + [swap(hidden, k) for k in range(1, TPE)]
    (result,) = call(
        down_kernel, [((rows, quarter), BF16)], *hiddens, *weights,
        flops=2 * rows * width * units,
    )
    returned = over_y(result)
    kept, *halves = call(
        combine_kernel,
        [((tok, block), F32)] + [((tok, block), BF16)] * (TPE - 1),
        place, high, low, returned,
    )
    halves = [swap(h, TPE * (k + 1)) for k, h in enumerate(halves)]
    (mixed,) = call(finish_kernel, [((tok, block), BF16)], kept, *halves)
    return mixed


def solution(mesh):
    return jax.shard_map(
        on_device,
        mesh=mesh,
        in_specs=(
            P(("grp", "side"), None),
            P(("grp", "side"), None),
            P(("grp", "side"), None),
            P(("grp", "shard"), None, None),
            P(("grp", "shard"), None, None),
            P(("grp", "shard"), None, None),
        ),
        out_specs=P(("grp", "side"), "shard"),
        check_vma=False,
    )
```

```python
import functools

import jax
import jax.numpy as jnp
from jax import lax
from jax.experimental import pallas as pl
from jax.experimental.pallas import tpu as pltpu
from jax.sharding import PartitionSpec as P


TPE = 4
BF16 = jnp.bfloat16
F32 = jnp.float32


def dot(a, b, dims=((1,), (0,))):
    return lax.dot_general(a, b, (dims, ((), ())), preferred_element_type=F32)


def dispatch_kernel(cap, per_group, place, routes, probs, tokens, *outs):
    tok = tokens.shape[0]
    rows = outs[0].shape[0]
    half = cap // 2
    gates = probs[...] / jnp.sum(probs[...], axis=0, keepdims=True)
    before = lax.broadcasted_iota(jnp.int32, (tok, tok), 0)
    before = before < lax.broadcasted_iota(jnp.int32, (tok, tok), 1)
    before = jnp.where(before, F32(1.0), F32(0.0)).astype(BF16)
    row = lax.broadcasted_iota(jnp.int32, (rows, tok), 0)
    target = lax.shift_right_logical(row, half.bit_length() - 1) * per_group + place[0]
    slot = lax.bitwise_and(row, half - 1).astype(F32)
    hits = jnp.zeros((rows, tok), F32)
    weight = jnp.zeros((rows, tok), F32)
    for k in range(routes.shape[0]):
        match = routes[k : k + 1, :] == target
        hits = jnp.where(match, F32(1.0), hits)
        weight = jnp.where(match, gates[k : k + 1, :], weight)
    ranks = dot(hits.astype(BF16), before)
    for part in range(2):
        sent, high, low = outs[3 * part : 3 * part + 3]
        chosen = (hits > 0.5) & (ranks == slot + F32(part * half))
        select = jnp.where(chosen, F32(1.0), F32(0.0)).astype(BF16)
        mine = jnp.where(chosen, weight, F32(0.0))
        top = mine.astype(BF16)
        high[...] = top
        low[...] = (mine - top.astype(F32)).astype(BF16)
        width = sent.shape[1]
        step = min(512, width)
        for at in range(0, width, step):
            start = place[2] * width + at if part == 0 else at
            piece = tokens[:, pl.ds(pl.multiple_of(start, step), step)]
            sent[:, at : at + step] = dot(select, piece).astype(BF16)


def shuffle_kernel(block, place, weights, *outs):
    for k, out in enumerate(outs):
        owner = lax.bitwise_xor(place[1], k)
        for m in range(out.shape[1] // block):
            at = pl.multiple_of((m * TPE + owner) * block, block)
            out[:, m * block : (m + 1) * block] = weights[:, pl.ds(at, block)]


def activate(gate, upper):
    return (gate / (1.0 + jnp.exp(-gate)) * upper).astype(BF16)


def hidden_pair_kernel(place, mine, other, w_gate, w_up, out):
    width = mine.shape[1]
    own = pl.ds(pl.multiple_of(place[2] * width, width), width)
    far = pl.ds(pl.multiple_of((1 - place[2]) * width, width), width)
    gate = dot(mine[...], w_gate[own, :]) + dot(other[...], w_gate[far, :])
    upper = dot(mine[...], w_up[own, :]) + dot(other[...], w_up[far, :])
    out[...] = activate(gate, upper)


def hidden_kernel(rows, w_gate, w_up, out):
    out[...] = activate(dot(rows[...], w_gate[...]), dot(rows[...], w_up[...]))


def down_kernel(*refs):
    weights, out = refs[2 * TPE : 3 * TPE], refs[-1]
    groups, cap, width = out.shape
    step = min(256, width)
    for part in range(2):
        hidden = refs[part * TPE : (part + 1) * TPE]
        slots = slice(part * cap // 2, (part + 1) * cap // 2)
        for at in range(0, width, step):
            total = dot(hidden[0][...], weights[0][:, at : at + step])
            for k in range(1, TPE):
                total = total + dot(hidden[k][...], weights[k][:, at : at + step])
            total = total.reshape(groups, cap // 2, step)
            out[:, slots, at : at + step] = total.astype(BF16)


def combine_kernel(place, high_a, low_a, high_b, low_b, rows, kept, *sent):
    block = kept.shape[1]
    groups, cap, _ = rows.shape
    for k in range(TPE):
        at = pl.multiple_of(lax.bitwise_xor(place[0], k) * block, block)
        total = jnp.zeros(kept.shape, F32)
        for part, pair in enumerate(((high_a, low_a), (high_b, low_b))):
            slots = slice(part * cap // 2, (part + 1) * cap // 2)
            piece = rows[:, slots, pl.ds(at, block)].astype(F32)
            piece = piece.reshape(groups * cap // 2, block).astype(BF16)
            for factor in pair:
                total = total + dot(factor[...], piece, ((0,), (0,)))
        if k == 0:
            kept[...] = total
        else:
            sent[k - 1][...] = total.astype(BF16)


def finish_kernel(kept, *refs):
    total = kept[...]
    for part in refs[:-1]:
        total = total + part[...].astype(F32)
    refs[-1][...] = total.astype(BF16)


def call(kernel, shapes, *args, flops=0, limit=None):
    specs = [pl.BlockSpec(memory_space=pltpu.VMEM)] * len(args)
    if args[0].ndim == 1:
        specs[0] = pl.BlockSpec(memory_space=pltpu.SMEM)
    outs = [jax.ShapeDtypeStruct(s, d) for s, d in shapes]
    moved = sum(a.size * a.dtype.itemsize for a in (*args, *outs))
    return pl.pallas_call(
        kernel,
        out_shape=outs,
        in_specs=specs,
        out_specs=[pl.BlockSpec(memory_space=pltpu.VMEM)] * len(outs),
        compiler_params=pltpu.CompilerParams(vmem_limit_bytes=limit),
        cost_estimate=pl.CostEstimate(flops=flops, bytes_accessed=moved, transcendentals=0),
    )(*args)


def on_device(tokens, routes, probs, w_gate, w_up, w_down):
    groups, shards = lax.axis_size("grp"), lax.axis_size("shard")
    per_group = shards // TPE
    tok, width = tokens.shape
    units = w_down.shape[1]
    block, quarter = width // shards, width // TPE
    cap = 2 * tok * routes.shape[1] // (groups * per_group)
    rows = groups * cap // 2
    room = 16 << 20
    z = lax.axis_index("shard")
    place = jnp.stack([z // TPE, lax.rem(z, TPE), lax.rem(z, 2)]).astype(jnp.int32)

    def over_y(x):
        return lax.all_to_all(x.reshape(groups, -1, x.shape[-1]), "grp", 0, 0, tiled=True)

    def swap(x, bits):
        return lax.ppermute(x, "shard", [(i, i ^ bits) for i in range(shards)])

    factor = ((rows, tok), BF16)
    sent_a, high_a, low_a, sent_b, high_b, low_b = call(
        functools.partial(dispatch_kernel, cap, per_group),
        [((rows, width // 2), BF16), factor, factor, ((rows, width), BF16), factor, factor],
        place, routes.T, probs.T, tokens, flops=3 * rows * tok * width,
    )
    mine = over_y(sent_a).reshape(rows, width // 2)
    parts = call(
        functools.partial(shuffle_kernel, block),
        [((units, quarter), BF16)] * TPE, place, w_down[0],
    )
    weights = [parts[0]] + [swap(parts[k], k) for k in range(1, TPE)]
    other = swap(mine, 1)
    arrived = over_y(sent_b).reshape(rows, width)
    (hidden_a,) = call(
        hidden_pair_kernel, [((rows, units), BF16)], place, mine, other, w_gate[0], w_up[0],
        flops=4 * rows * width * units,
    )
    hiddens_a = [hidden_a] + [swap(hidden_a, k) for k in range(1, TPE)]
    (hidden_b,) = call(
        hidden_kernel, [((rows, units), BF16)], arrived, w_gate[0], w_up[0],
        flops=4 * rows * width * units, limit=room,
    )
    hiddens_b = [hidden_b] + [swap(hidden_b, k) for k in range(1, TPE)]
    (result,) = call(
        down_kernel, [((groups, cap, quarter), BF16)], *hiddens_a, *hiddens_b, *weights,
        flops=4 * rows * width * units, limit=room,
    )
    returned = over_y(result)
    kept, *halves = call(
        combine_kernel,
        [((tok, block), F32)] + [((tok, block), BF16)] * (TPE - 1),
        place, high_a, low_a, high_b, low_b, returned, limit=room,
    )
    halves = [swap(h, TPE * (k + 1)) for k, h in enumerate(halves)]
    (mixed,) = call(finish_kernel, [((tok, block), BF16)], kept, *halves, limit=room)
    return mixed


def solution(mesh):
    return jax.shard_map(
        on_device,
        mesh=mesh,
        in_specs=(
            P(("grp", "side"), None),
            P(("grp", "side"), None),
            P(("grp", "side"), None),
            P(("grp", "shard"), None, None),
            P(("grp", "shard"), None, None),
            P(("grp", "shard"), None, None),
        ),
        out_specs=P(("grp", "side"), "shard"),
        check_vma=False,
    )
```

```python
import functools

import jax
import jax.numpy as jnp
from jax import lax
from jax.experimental import pallas as pl
from jax.experimental.pallas import tpu as pltpu
from jax.sharding import PartitionSpec as P


TPE = 4
BF16 = jnp.bfloat16
F32 = jnp.float32


def dot(a, b, dims=((1,), (0,))):
    return lax.dot_general(a, b, (dims, ((), ())), preferred_element_type=F32)


def dispatch_kernel(cap, per_group, place, routes, probs, tokens, *outs):
    tok = tokens.shape[0]
    rows = outs[0].shape[0]
    half = cap // 2
    gates = probs[...] / jnp.sum(probs[...], axis=0, keepdims=True)
    before = lax.broadcasted_iota(jnp.int32, (tok, tok), 0)
    before = before < lax.broadcasted_iota(jnp.int32, (tok, tok), 1)
    before = jnp.where(before, F32(1.0), F32(0.0)).astype(BF16)
    row = lax.broadcasted_iota(jnp.int32, (rows, tok), 0)
    target = lax.shift_right_logical(row, half.bit_length() - 1) * per_group + place[0]
    slot = lax.bitwise_and(row, half - 1).astype(F32)
    hits = jnp.zeros((rows, tok), F32)
    weight = jnp.zeros((rows, tok), F32)
    for k in range(routes.shape[0]):
        match = routes[k : k + 1, :] == target
        hits = jnp.where(match, F32(1.0), hits)
        weight = jnp.where(match, gates[k : k + 1, :], weight)
    ranks = dot(hits.astype(BF16), before)
    for part in range(2):
        sent, high, low = outs[3 * part : 3 * part + 3]
        chosen = (hits > 0.5) & (ranks == slot + F32(part * half))
        select = jnp.where(chosen, F32(1.0), F32(0.0)).astype(BF16)
        mine = jnp.where(chosen, weight, F32(0.0))
        top = mine.astype(BF16)
        high[...] = top
        low[...] = (mine - top.astype(F32)).astype(BF16)
        width = sent.shape[1]
        step = min(512, width)
        for at in range(0, width, step):
            start = place[2] * width + at if part == 0 else at
            piece = tokens[:, pl.ds(pl.multiple_of(start, step), step)]
            sent[:, at : at + step] = dot(select, piece).astype(BF16)


def shuffle_kernel(block, place, weights, *outs):
    for k, out in enumerate(outs):
        at = place[3] * TPE + lax.bitwise_xor(place[1], k)
        out[...] = weights[:, pl.ds(pl.multiple_of(at * block, block), block)]


def stack_kernel(*refs):
    size = refs[0].shape[0]
    for k, ref in enumerate(refs[:-1]):
        refs[-1][k * size : (k + 1) * size, :] = ref[...]


def activate(gate, upper):
    return (gate / (1.0 + jnp.exp(-gate)) * upper).astype(BF16)


def hidden_pair_kernel(place, mine, other, w_gate, w_up, out):
    width = mine.shape[1]
    own = pl.ds(pl.multiple_of(place[2] * width, width), width)
    far = pl.ds(pl.multiple_of((1 - place[2]) * width, width), width)
    gate = dot(mine[...], w_gate[own, :]) + dot(other[...], w_gate[far, :])
    upper = dot(mine[...], w_up[own, :]) + dot(other[...], w_up[far, :])
    out[...] = activate(gate, upper)


def hidden_kernel(rows, w_gate, w_up, out):
    out[...] = activate(dot(rows[...], w_gate[...]), dot(rows[...], w_up[...]))


def down_kernel(place, *refs):
    weights, out = refs[2 * TPE : -1], refs[-1]
    groups, cap, _ = out.shape
    block = weights[0].shape[1]
    units = refs[0].shape[1]
    for part in range(2):
        hidden = refs[part * TPE : (part + 1) * TPE]
        slots = slice(part * cap // 2, (part + 1) * cap // 2)
        for side, weight in enumerate(weights):
            total = dot(hidden[0][...], weight[:units, :])
            for k in range(1, TPE):
                total = total + dot(hidden[k][...], weight[k * units : (k + 1) * units, :])
            total = total.reshape(groups, cap // 2, block).astype(BF16)
            at = pl.multiple_of(lax.bitwise_xor(place[3], side) * block, block)
            out[:, slots, pl.ds(at, block)] = total


def combine_kernel(place, high_a, low_a, high_b, low_b, rows, kept, *sent):
    block = kept.shape[1]
    groups, cap, _ = rows.shape
    for k in range(TPE):
        at = pl.multiple_of(lax.bitwise_xor(place[0], k) * block, block)
        total = jnp.zeros(kept.shape, F32)
        for part, pair in enumerate(((high_a, low_a), (high_b, low_b))):
            slots = slice(part * cap // 2, (part + 1) * cap // 2)
            piece = rows[:, slots, pl.ds(at, block)].astype(F32)
            piece = piece.reshape(groups * cap // 2, block).astype(BF16)
            for factor in pair:
                total = total + dot(factor[...], piece, ((0,), (0,)))
        if k == 0:
            kept[...] = total
        else:
            sent[k - 1][...] = total.astype(BF16)


def finish_kernel(kept, *refs):
    total = kept[...]
    for part in refs[:-1]:
        total = total + part[...].astype(F32)
    refs[-1][...] = total.astype(BF16)


def call(kernel, shapes, *args, flops=0, limit=None):
    specs = [pl.BlockSpec(memory_space=pltpu.VMEM)] * len(args)
    if args[0].ndim == 1:
        specs[0] = pl.BlockSpec(memory_space=pltpu.SMEM)
    outs = [jax.ShapeDtypeStruct(s, d) for s, d in shapes]
    moved = sum(a.size * a.dtype.itemsize for a in (*args, *outs))
    return pl.pallas_call(
        kernel,
        out_shape=outs,
        in_specs=specs,
        out_specs=[pl.BlockSpec(memory_space=pltpu.VMEM)] * len(outs),
        compiler_params=pltpu.CompilerParams(vmem_limit_bytes=limit),
        cost_estimate=pl.CostEstimate(flops=flops, bytes_accessed=moved, transcendentals=0),
    )(*args)


def on_device(tokens, routes, probs, w_gate, w_up, w_down):
    groups, shards = lax.axis_size("grp"), lax.axis_size("shard")
    per_group = shards // TPE
    tok, width = tokens.shape
    units = w_down.shape[1]
    block, quarter = width // shards, width // TPE
    cap = 2 * tok * routes.shape[1] // (groups * per_group)
    rows = groups * cap // 2
    room = 16 << 20
    z = lax.axis_index("shard")
    sides = lax.axis_size("side")
    place = [z // TPE, lax.rem(z, TPE), lax.rem(z, 2), lax.axis_index("side")]
    place = jnp.stack(place).astype(jnp.int32)

    def over_y(x):
        return lax.all_to_all(x.reshape(groups, -1, x.shape[-1]), "grp", 0, 0, tiled=True)

    def swap(x, bits, axis="shard"):
        return lax.ppermute(x, axis, [(i, i ^ bits) for i in range(lax.axis_size(axis))])

    factor = ((rows, tok), BF16)
    sent_a, high_a, low_a, sent_b, high_b, low_b = call(
        functools.partial(dispatch_kernel, cap, per_group),
        [((rows, width // 2), BF16), factor, factor, ((rows, width), BF16), factor, factor],
        place, routes.T, probs.T, tokens, flops=3 * rows * tok * width,
    )
    mine = over_y(sent_a).reshape(rows, width // 2)
    parts = call(
        functools.partial(shuffle_kernel, block),
        [((units, block), BF16)] * TPE, place, w_down[0],
    )
    parts = [parts[0]] + [swap(parts[k], k) for k in range(1, TPE)]
    (weight,) = call(stack_kernel, [((units * TPE, block), BF16)], *parts)
    weights = [weight] + [swap(weight, k, "side") for k in range(1, sides)]
    other = swap(mine, 1)
    arrived = over_y(sent_b).reshape(rows, width)
    (hidden_a,) = call(
        hidden_pair_kernel, [((rows, units), BF16)], place, mine, other, w_gate[0], w_up[0],
        flops=4 * rows * width * units,
    )
    hiddens_a = [hidden_a] + [swap(hidden_a, k) for k in range(1, TPE)]
    (hidden_b,) = call(
        hidden_kernel, [((rows, units), BF16)], arrived, w_gate[0], w_up[0],
        flops=4 * rows * width * units, limit=room,
    )
    hiddens_b = [hidden_b] + [swap(hidden_b, k) for k in range(1, TPE)]
    (result,) = call(
        down_kernel, [((groups, cap, quarter), BF16)],
        place, *hiddens_a, *hiddens_b, *weights,
        flops=4 * rows * width * units, limit=room,
    )
    returned = over_y(result)
    kept, *halves = call(
        combine_kernel,
        [((tok, block), F32)] + [((tok, block), BF16)] * (TPE - 1),
        place, high_a, low_a, high_b, low_b, returned, limit=room,
    )
    halves = [swap(h, TPE * (k + 1)) for k, h in enumerate(halves)]
    (mixed,) = call(finish_kernel, [((tok, block), BF16)], kept, *halves, limit=room)
    return mixed


def solution(mesh):
    return jax.shard_map(
        on_device,
        mesh=mesh,
        in_specs=(
            P(("grp", "side"), None),
            P(("grp", "side"), None),
            P(("grp", "side"), None),
            P(("grp", "shard"), None, None),
            P(("grp", "shard"), None, None),
            P(("grp", "shard"), None, None),
        ),
        out_specs=P(("grp", "side"), "shard"),
        check_vma=False,
    )
```

```python
import functools

import jax
import jax.numpy as jnp
from jax import lax
from jax.experimental import pallas as pl
from jax.experimental.pallas import tpu as pltpu
from jax.sharding import PartitionSpec as P


TPE = 4
BF16 = jnp.bfloat16
F32 = jnp.float32


def dot(a, b, dims=((1,), (0,))):
    return lax.dot_general(a, b, (dims, ((), ())), preferred_element_type=F32)


def unpack(place):
    z = lax.shift_right_logical(place[0], 2)
    quartet, tile = lax.shift_right_logical(z, 2), lax.bitwise_and(z, 3)
    return quartet, tile, lax.bitwise_and(z, 1), lax.bitwise_and(place[0], 3)


def dispatch_kernel(cap, per_group, part, place, routes, probs, tokens, sent, high, low):
    tok = tokens.shape[0]
    rows, width = sent.shape
    half = cap // 2
    gates = probs[...] / jnp.sum(probs[...], axis=0, keepdims=True)
    before = lax.broadcasted_iota(jnp.int32, (tok, tok), 0)
    before = before < lax.broadcasted_iota(jnp.int32, (tok, tok), 1)
    before = jnp.where(before, F32(1.0), F32(0.0)).astype(BF16)
    row = lax.broadcasted_iota(jnp.int32, (rows, tok), 0)
    target = lax.shift_right_logical(row, half.bit_length() - 1) * per_group + unpack(place)[0]
    slot = (lax.bitwise_and(row, half - 1) + part * half).astype(F32)
    hits = jnp.zeros((rows, tok), F32)
    weight = jnp.zeros((rows, tok), F32)
    for k in range(routes.shape[0]):
        match = routes[k : k + 1, :] == target
        hits = jnp.where(match, F32(1.0), hits)
        weight = jnp.where(match, gates[k : k + 1, :], weight)
    ranks = dot(hits.astype(BF16), before)
    chosen = (hits > 0.5) & (ranks == slot)
    select = jnp.where(chosen, F32(1.0), F32(0.0)).astype(BF16)
    mine = jnp.where(chosen, weight, F32(0.0))
    top = mine.astype(BF16)
    high[...] = top
    low[...] = (mine - top.astype(F32)).astype(BF16)
    step = min(512, width)
    for at in range(0, width, step):
        start = unpack(place)[2] * width + at if part == 0 else at
        piece = tokens[:, pl.ds(pl.multiple_of(start, step), step)]
        sent[:, at : at + step] = dot(select, piece).astype(BF16)


def shuffle_kernel(block, place, weights, *outs):
    for k, out in enumerate(outs):
        at = unpack(place)[3] * TPE + lax.bitwise_xor(unpack(place)[1], k)
        out[...] = weights[:, pl.ds(pl.multiple_of(at * block, block), block)]


def stack_kernel(*refs):
    size = refs[0].shape[0]
    for k, ref in enumerate(refs[:-1]):
        refs[-1][k * size : (k + 1) * size, :] = ref[...]


def activate(gate, upper):
    return (gate / (1.0 + jnp.exp(-gate)) * upper).astype(BF16)


def hidden_kernel(count, place, *refs):
    rows, w_gate, w_up = refs[:count], refs[count : 2 * count], refs[2 * count : 3 * count]
    out, gate, upper = refs[3 * count :]
    step = pl.program_id(0)
    if count == 1:
        size = w_gate[0].shape[0]
        piece = rows[0][:, pl.ds(pl.multiple_of(step * size, size), size)]
        gates, uppers = dot(piece, w_gate[0][...]), dot(piece, w_up[0][...])
    else:
        gates = dot(rows[0][...], w_gate[0][...]) + dot(rows[1][...], w_gate[1][...])
        uppers = dot(rows[0][...], w_up[0][...]) + dot(rows[1][...], w_up[1][...])

    @pl.when(step == 0)
    def _():
        gate[...] = gates
        upper[...] = uppers

    @pl.when(step > 0)
    def _():
        gate[...] += gates
        upper[...] += uppers

    @pl.when(step == pl.num_programs(0) - 1)
    def _():
        out[...] = activate(gate[...], upper[...])


def gate_up(place, rows, w_gate, w_up, steps=4):
    count, (height, width) = len(rows), rows[0].shape
    units, step = w_gate.shape[1], width // steps

    def near(i, place):
        return (i + steps * unpack(place)[2] if count == 2 else i, 0)

    def far(i, place):
        return (i + steps * (1 - unpack(place)[2]), 0)

    maps = [near, far][:count]
    row_spec = pl.BlockSpec((height, step), lambda i, place: (0, i))
    if count == 1:
        row_spec = pl.BlockSpec(memory_space=pltpu.VMEM)
        rows = [pltpu.with_memory_space_constraint(rows[0], pltpu.VMEM)]
    return pl.pallas_call(
        functools.partial(hidden_kernel, count),
        out_shape=jax.ShapeDtypeStruct((height, units), BF16),
        grid_spec=pltpu.PrefetchScalarGridSpec(
            num_scalar_prefetch=1,
            grid=(steps,),
            in_specs=[row_spec] * count
            + [pl.BlockSpec((step, units), m) for m in maps] * 2,
            out_specs=pl.BlockSpec(memory_space=pltpu.VMEM),
            scratch_shapes=[pltpu.VMEM((height, units), F32)] * 2,
        ),
        cost_estimate=pl.CostEstimate(
            flops=4 * height * units * w_gate.shape[0],
            bytes_accessed=4 * w_gate.size,
            transcendentals=height * units,
        ),
    )(place, *rows, *[w_gate] * count, *[w_up] * count)


def down_kernel(place, hidden, *refs):
    weights, out = refs[:-1], refs[-1]
    groups, cap, _ = out.shape
    block = weights[0].shape[1]
    count, height, units = hidden.shape
    _, tile, _, own_side = unpack(place)
    for side, weight in enumerate(weights):
        total = jnp.zeros((height, block), F32)
        for k in range(count):
            rows = hidden[lax.bitwise_xor(tile, k)]
            total = total + dot(rows, weight[k * units : (k + 1) * units, :])
        at = pl.multiple_of(lax.bitwise_xor(own_side, side) * block, block)
        total = total.reshape(2, groups, cap // 2, block).astype(BF16)
        for part in range(2):
            slots = slice(part * cap // 2, (part + 1) * cap // 2)
            out[:, slots, pl.ds(at, block)] = total[part]


def combine_kernel(high_a, low_a, high_b, low_b, rows, out):
    count, tok, block = out.shape
    groups, cap, _ = rows.shape
    for k in range(count):
        total = jnp.zeros((tok, block), F32)
        for part, pair in enumerate(((high_a, low_a), (high_b, low_b))):
            slots = slice(part * cap // 2, (part + 1) * cap // 2)
            piece = rows[:, slots, k * block : (k + 1) * block].astype(F32)
            piece = piece.reshape(groups * cap // 2, block).astype(BF16)
            for factor in pair:
                total = total + dot(factor[...], piece, ((0,), (0,)))
        out[k] = total.astype(BF16)


def finish_kernel(parts, out):
    total = parts[0].astype(F32)
    for k in range(1, parts.shape[0]):
        total = total + parts[k].astype(F32)
    out[...] = total.astype(BF16)


def call(kernel, shapes, *args, flops=0, limit=None):
    specs = [pl.BlockSpec(memory_space=pltpu.VMEM)] * len(args)
    if args[0].ndim == 1:
        specs[0] = pl.BlockSpec(memory_space=pltpu.SMEM)
    outs = [jax.ShapeDtypeStruct(s, d) for s, d in shapes]
    moved = sum(a.size * a.dtype.itemsize for a in (*args, *outs))
    return pl.pallas_call(
        kernel,
        out_shape=outs,
        in_specs=specs,
        out_specs=[pl.BlockSpec(memory_space=pltpu.VMEM)] * len(outs),
        compiler_params=pltpu.CompilerParams(vmem_limit_bytes=limit),
        cost_estimate=pl.CostEstimate(flops=flops, bytes_accessed=moved, transcendentals=0),
    )(*args)


def on_device(tokens, routes, probs, w_gate, w_up, w_down):
    groups, shards = lax.axis_size("grp"), lax.axis_size("shard")
    per_group = shards // TPE
    tok, width = tokens.shape
    units = w_down.shape[1]
    block, quarter = width // shards, width // TPE
    cap = 2 * tok * routes.shape[1] // (groups * per_group)
    rows = groups * cap // 2
    room = 16 << 20
    z = lax.axis_index("shard")
    sides = lax.axis_size("side")
    place = (z * TPE + lax.axis_index("side")).astype(jnp.int32).reshape(1)

    def over_y(x):
        return lax.all_to_all(x.reshape(groups, -1, x.shape[-1]), "grp", 0, 0, tiled=True)

    def swap(x, bits, axis="shard"):
        return lax.ppermute(x, axis, [(i, i ^ bits) for i in range(lax.axis_size(axis))])

    factor = ((rows, tok), BF16)

    def dispatch(part, size):
        return call(
            functools.partial(dispatch_kernel, cap, per_group, part),
            [((rows, size), BF16), factor, factor],
            place, routes.T, probs.T, tokens, flops=2 * rows * tok * size,
        )

    sent_a, high_a, low_a = dispatch(0, width // 2)
    mine = over_y(sent_a).reshape(rows, width // 2)
    sent_b, high_b, low_b = dispatch(1, width)
    parts = call(
        functools.partial(shuffle_kernel, block),
        [((units, block), BF16)] * TPE, place, w_down[0],
    )
    parts = [parts[0]] + [swap(parts[k], k) for k in range(1, TPE)]
    (weight,) = call(stack_kernel, [((units * TPE, block), BF16)], *parts)
    weights = [weight] + [swap(weight, k, "side") for k in range(1, sides)]
    other = swap(mine, 1)
    arrived = over_y(sent_b).reshape(rows, width)
    hidden_a = gate_up(place, [mine, other], w_gate[0], w_up[0])
    hidden_b = gate_up(place, [arrived], w_gate[0], w_up[0])
    quartets = [[i * TPE + k for k in range(TPE)] for i in range(per_group)]
    strided = [[i * TPE + k for i in range(per_group)] for k in range(TPE)]
    hidden = jnp.concatenate([hidden_a, hidden_b], axis=0)
    hidden = lax.all_gather(hidden, "shard", axis_index_groups=quartets)
    (result,) = call(
        down_kernel, [((groups, cap, quarter), BF16)], place, hidden, *weights,
        flops=4 * rows * width * units, limit=room,
    )
    returned = over_y(result)
    (parts,) = call(
        combine_kernel, [((per_group, tok, block), BF16)],
        high_a, low_a, high_b, low_b, returned, limit=room,
    )
    parts = lax.all_to_all(parts, "shard", 0, 0, tiled=True, axis_index_groups=strided)
    (mixed,) = call(finish_kernel, [((tok, block), BF16)], parts, limit=room)
    return mixed


def solution(mesh):
    return jax.shard_map(
        on_device,
        mesh=mesh,
        in_specs=(
            P(("grp", "side"), None),
            P(("grp", "side"), None),
            P(("grp", "side"), None),
            P(("grp", "shard"), None, None),
            P(("grp", "shard"), None, None),
            P(("grp", "shard"), None, None),
        ),
        out_specs=P(("grp", "side"), "shard"),
        check_vma=False,
    )
```

```python
import functools

import jax
import jax.numpy as jnp
from jax import lax
from jax.experimental import pallas as pl
from jax.experimental.pallas import tpu as pltpu
from jax.sharding import PartitionSpec as P


TPE = 4
BF16 = jnp.bfloat16
F32 = jnp.float32


def dot(a, b, dims=((1,), (0,))):
    return lax.dot_general(a, b, (dims, ((), ())), preferred_element_type=F32)


def unpack(place):
    z = lax.shift_right_logical(place[0], 2)
    quartet, tile = lax.shift_right_logical(z, 2), lax.bitwise_and(z, 3)
    return quartet, tile, lax.bitwise_and(z, 1), lax.bitwise_and(place[0], 3)


def dispatch_kernel(cap, per_group, part, place, routes, probs, tokens, sent, high, low):
    tok = tokens.shape[0]
    rows, width = sent.shape
    half = cap // 2
    gates = probs[...] / jnp.sum(probs[...], axis=0, keepdims=True)
    before = lax.broadcasted_iota(jnp.int32, (tok, tok), 0)
    before = before < lax.broadcasted_iota(jnp.int32, (tok, tok), 1)
    before = jnp.where(before, F32(1.0), F32(0.0)).astype(BF16)
    row = lax.broadcasted_iota(jnp.int32, (rows, tok), 0)
    target = lax.shift_right_logical(row, half.bit_length() - 1) * per_group + unpack(place)[0]
    slot = (lax.bitwise_and(row, half - 1) + part * half).astype(F32)
    hits = jnp.zeros((rows, tok), F32)
    weight = jnp.zeros((rows, tok), F32)
    for k in range(routes.shape[0]):
        match = routes[k : k + 1, :] == target
        hits = jnp.where(match, F32(1.0), hits)
        weight = jnp.where(match, gates[k : k + 1, :], weight)
    ranks = dot(hits.astype(BF16), before)
    chosen = (hits > 0.5) & (ranks == slot)
    select = jnp.where(chosen, F32(1.0), F32(0.0)).astype(BF16)
    mine = jnp.where(chosen, weight, F32(0.0))
    top = mine.astype(BF16)
    high[...] = top
    low[...] = (mine - top.astype(F32)).astype(BF16)
    step = min(512, width)
    for at in range(0, width, step):
        start = unpack(place)[2] * width + at if part == 0 else at
        piece = tokens[:, pl.ds(pl.multiple_of(start, step), step)]
        sent[:, at : at + step] = dot(select, piece).astype(BF16)


def shuffle_kernel(block, place, weights, *outs):
    for k, out in enumerate(outs):
        at = unpack(place)[3] * TPE + lax.bitwise_xor(unpack(place)[1], k)
        out[...] = weights[:, pl.ds(pl.multiple_of(at * block, block), block)]


def stack_kernel(*refs):
    size = refs[0].shape[0]
    for k, ref in enumerate(refs[:-1]):
        refs[-1][k * size : (k + 1) * size, :] = ref[...]


def activate(gate, upper):
    return (gate / (1.0 + jnp.exp(-gate)) * upper).astype(BF16)


def hidden_a_kernel(place, mine, other, w_gate, w_up, out):
    width = mine.shape[1]
    parity = unpack(place)[2]
    own = pl.ds(pl.multiple_of(parity * width, width), width)
    far = pl.ds(pl.multiple_of((1 - parity) * width, width), width)
    gate = dot(mine[...], w_gate[own, :]) + dot(other[...], w_gate[far, :])
    upper = dot(mine[...], w_up[own, :]) + dot(other[...], w_up[far, :])
    out[...] = activate(gate, upper)


def hidden_b_kernel(before, rows, w_gate, w_up_far, out, w_up, sems):
    height = before.shape[0]
    load = pltpu.make_async_copy(w_up_far, w_up, sems.at[0])
    load.start()
    keep = pltpu.make_async_copy(before, out.at[pl.ds(0, height), :], sems.at[1])
    keep.start()
    gate = dot(rows[...], w_gate[...])
    keep.wait()
    load.wait()
    out[height:, :] = activate(gate, dot(rows[...], w_up[...]))


def hidden_b(before, rows, w_gate, w_up):
    height, units = before.shape
    inside = pl.BlockSpec(memory_space=pltpu.VMEM)
    outside = pl.BlockSpec(memory_space=pltpu.HBM)
    before = pltpu.with_memory_space_constraint(before, pltpu.HBM)
    return pl.pallas_call(
        hidden_b_kernel,
        out_shape=jax.ShapeDtypeStruct((2 * height, units), BF16),
        in_specs=[outside, inside, inside, outside],
        out_specs=inside,
        scratch_shapes=[pltpu.VMEM(w_up.shape, BF16), pltpu.SemaphoreType.DMA((2,))],
        compiler_params=pltpu.CompilerParams(vmem_limit_bytes=16 << 20),
        cost_estimate=pl.CostEstimate(
            flops=4 * height * w_up.size, bytes_accessed=4 * w_up.size, transcendentals=0
        ),
    )(before, rows, w_gate, pltpu.with_memory_space_constraint(w_up, pltpu.HBM))


def down_kernel(place, hidden, *refs):
    weights, out = refs[:-1], refs[-1]
    groups, cap, _ = out.shape
    block = weights[0].shape[1]
    count, height, units = hidden.shape
    _, tile, _, own_side = unpack(place)
    for side, weight in enumerate(weights):
        total = jnp.zeros((height, block), F32)
        for k in range(count):
            rows = hidden[lax.bitwise_xor(tile, k)]
            total = total + dot(rows, weight[k * units : (k + 1) * units, :])
        at = pl.multiple_of(lax.bitwise_xor(own_side, side) * block, block)
        total = total.reshape(2, groups, cap // 2, block).astype(BF16)
        for part in range(2):
            slots = slice(part * cap // 2, (part + 1) * cap // 2)
            out[:, slots, pl.ds(at, block)] = total[part]


def combine_kernel(high_a, low_a, high_b, low_b, rows, out):
    count, tok, block = out.shape
    groups, cap, _ = rows.shape
    for k in range(count):
        total = jnp.zeros((tok, block), F32)
        for part, pair in enumerate(((high_a, low_a), (high_b, low_b))):
            slots = slice(part * cap // 2, (part + 1) * cap // 2)
            piece = rows[:, slots, k * block : (k + 1) * block].astype(F32)
            piece = piece.reshape(groups * cap // 2, block).astype(BF16)
            for factor in pair:
                total = total + dot(factor[...], piece, ((0,), (0,)))
        out[k] = total.astype(BF16)


def finish_kernel(parts, out):
    total = parts[0].astype(F32)
    for k in range(1, parts.shape[0]):
        total = total + parts[k].astype(F32)
    out[...] = total.astype(BF16)


def call(kernel, shapes, *args, flops=0, limit=None):
    specs = [pl.BlockSpec(memory_space=pltpu.VMEM)] * len(args)
    if args[0].ndim == 1:
        specs[0] = pl.BlockSpec(memory_space=pltpu.SMEM)
    outs = [jax.ShapeDtypeStruct(s, d) for s, d in shapes]
    moved = sum(a.size * a.dtype.itemsize for a in (*args, *outs))
    return pl.pallas_call(
        kernel,
        out_shape=outs,
        in_specs=specs,
        out_specs=[pl.BlockSpec(memory_space=pltpu.VMEM)] * len(outs),
        compiler_params=pltpu.CompilerParams(vmem_limit_bytes=limit),
        cost_estimate=pl.CostEstimate(flops=flops, bytes_accessed=moved, transcendentals=0),
    )(*args)


def on_device(tokens, routes, probs, w_gate, w_up, w_down):
    groups, shards = lax.axis_size("grp"), lax.axis_size("shard")
    per_group = shards // TPE
    tok, width = tokens.shape
    units = w_down.shape[1]
    block, quarter = width // shards, width // TPE
    cap = 2 * tok * routes.shape[1] // (groups * per_group)
    rows = groups * cap // 2
    room = 16 << 20
    z = lax.axis_index("shard")
    sides = lax.axis_size("side")
    place = (z * TPE + lax.axis_index("side")).astype(jnp.int32).reshape(1)

    def over_y(x):
        return lax.all_to_all(x.reshape(groups, -1, x.shape[-1]), "grp", 0, 0, tiled=True)

    def swap(x, bits, axis="shard"):
        return lax.ppermute(x, axis, [(i, i ^ bits) for i in range(lax.axis_size(axis))])

    factor = ((rows, tok), BF16)

    def dispatch(part, size):
        return call(
            functools.partial(dispatch_kernel, cap, per_group, part),
            [((rows, size), BF16), factor, factor],
            place, routes.T, probs.T, tokens, flops=2 * rows * tok * size,
        )

    sent_a, high_a, low_a = dispatch(0, width // 2)
    mine = over_y(sent_a).reshape(rows, width // 2)
    sent_b, high_b, low_b = dispatch(1, width)
    parts = call(
        functools.partial(shuffle_kernel, block),
        [((units, block), BF16)] * TPE, place, w_down[0],
    )
    parts = [parts[0]] + [swap(parts[k], k) for k in range(1, TPE)]
    (weight,) = call(stack_kernel, [((units * TPE, block), BF16)], *parts)
    weights = [weight] + [swap(weight, k, "side") for k in range(1, sides)]
    other = swap(mine, 1)
    arrived = over_y(sent_b).reshape(rows, width)
    (hidden,) = call(
        hidden_a_kernel, [((rows, units), BF16)], place, mine, other, w_gate[0], w_up[0],
        flops=4 * rows * width * units,
    )
    hidden = hidden_b(hidden, arrived, w_gate[0], w_up[0])
    quartets = [[i * TPE + k for k in range(TPE)] for i in range(per_group)]
    strided = [[i * TPE + k for i in range(per_group)] for k in range(TPE)]
    hidden = lax.all_gather(hidden, "shard", axis_index_groups=quartets)
    (result,) = call(
        down_kernel, [((groups, cap, quarter), BF16)], place, hidden, *weights,
        flops=4 * rows * width * units, limit=room,
    )
    returned = over_y(result)
    (parts,) = call(
        combine_kernel, [((per_group, tok, block), BF16)],
        high_a, low_a, high_b, low_b, returned, limit=room,
    )
    parts = lax.all_to_all(parts, "shard", 0, 0, tiled=True, axis_index_groups=strided)
    (mixed,) = call(finish_kernel, [((tok, block), BF16)], parts, limit=room)
    return mixed


def solution(mesh):
    return jax.shard_map(
        on_device,
        mesh=mesh,
        in_specs=(
            P(("grp", "side"), None),
            P(("grp", "side"), None),
            P(("grp", "side"), None),
            P(("grp", "shard"), None, None),
            P(("grp", "shard"), None, None),
            P(("grp", "shard"), None, None),
        ),
        out_specs=P(("grp", "side"), "shard"),
        check_vma=False,
    )
```

```python
import functools

import jax
import jax.numpy as jnp
from jax import lax
from jax.experimental import pallas as pl
from jax.experimental.pallas import tpu as pltpu
from jax.sharding import PartitionSpec as P


TPE = 4
BF16 = jnp.bfloat16
F32 = jnp.float32


def dot(a, b, dims=((1,), (0,))):
    return lax.dot_general(a, b, (dims, ((), ())), preferred_element_type=F32)


def unpack(place):
    z = lax.shift_right_logical(place[0], 2)
    quartet, tile = lax.shift_right_logical(z, 2), lax.bitwise_and(z, 3)
    return quartet, tile, lax.bitwise_and(z, 1), lax.bitwise_and(place[0], 3)


def dispatch_kernel(cap, per_group, part, place, routes, probs, tokens, sent, high, low):
    tok = tokens.shape[0]
    rows, width = sent.shape
    half = cap // 2
    gates = probs[...] / jnp.sum(probs[...], axis=0, keepdims=True)
    before = lax.broadcasted_iota(jnp.int32, (tok, tok), 0)
    before = before < lax.broadcasted_iota(jnp.int32, (tok, tok), 1)
    before = jnp.where(before, F32(1.0), F32(0.0)).astype(BF16)
    row = lax.broadcasted_iota(jnp.int32, (rows, tok), 0)
    target = lax.shift_right_logical(row, half.bit_length() - 1) * per_group + unpack(place)[0]
    slot = (lax.bitwise_and(row, half - 1) + part * half).astype(F32)
    hits = jnp.zeros((rows, tok), F32)
    weight = jnp.zeros((rows, tok), F32)
    for k in range(routes.shape[0]):
        match = routes[k : k + 1, :] == target
        hits = jnp.where(match, F32(1.0), hits)
        weight = jnp.where(match, gates[k : k + 1, :], weight)
    ranks = dot(hits.astype(BF16), before)
    chosen = (hits > 0.5) & (ranks == slot)
    select = jnp.where(chosen, F32(1.0), F32(0.0)).astype(BF16)
    mine = jnp.where(chosen, weight, F32(0.0))
    top = mine.astype(BF16)
    high[...] = top
    low[...] = (mine - top.astype(F32)).astype(BF16)
    step = min(512, width)
    for at in range(0, width, step):
        start = unpack(place)[2] * width + at if part == 0 else at
        piece = tokens[:, pl.ds(pl.multiple_of(start, step), step)]
        sent[:, at : at + step] = dot(select, piece).astype(BF16)


def shuffle_kernel(place, weights, *refs):
    outs, sems = refs[:-1], refs[-1]
    _, tile, _, side = unpack(place)
    block = outs[0].shape[1]
    loads = []
    for k, out in enumerate(outs):
        at = pl.multiple_of((side * TPE + lax.bitwise_xor(tile, k)) * block, block)
        loads.append(pltpu.make_async_copy(weights.at[:, pl.ds(at, block)], out, sems.at[k]))
    for load in loads:
        load.start()
    for load in loads:
        load.wait()


def shuffle(place, weights, block):
    return pl.pallas_call(
        shuffle_kernel,
        out_shape=[jax.ShapeDtypeStruct((weights.shape[0], block), BF16)] * TPE,
        in_specs=[pl.BlockSpec(memory_space=pltpu.SMEM), pl.BlockSpec(memory_space=pltpu.HBM)],
        out_specs=[pl.BlockSpec(memory_space=pltpu.VMEM)] * TPE,
        scratch_shapes=[pltpu.SemaphoreType.DMA((TPE,))],
        compiler_params=pltpu.CompilerParams(vmem_limit_bytes=16 << 20),
        cost_estimate=pl.CostEstimate(
            flops=0, bytes_accessed=4 * TPE * weights.shape[0] * block, transcendentals=0
        ),
    )(place, pltpu.with_memory_space_constraint(weights, pltpu.HBM))


def stack_kernel(*refs):
    size = refs[0].shape[0]
    for k, ref in enumerate(refs[:-1]):
        refs[-1][k * size : (k + 1) * size, :] = ref[...]


def activate(gate, upper):
    return (gate / (1.0 + jnp.exp(-gate)) * upper).astype(BF16)


def hidden_a_kernel(place, mine, other, w_gate, w_up, out):
    width = mine.shape[1]
    parity = unpack(place)[2]
    own = pl.ds(pl.multiple_of(parity * width, width), width)
    far = pl.ds(pl.multiple_of((1 - parity) * width, width), width)
    gate = dot(mine[...], w_gate[own, :]) + dot(other[...], w_gate[far, :])
    upper = dot(mine[...], w_up[own, :]) + dot(other[...], w_up[far, :])
    out[...] = activate(gate, upper)


def hidden_b_kernel(before, rows, w_gate_far, w_up_far, out, w_gate, w_up, sems):
    height, pieces = before.shape[0], sems.shape[0] // 2
    size = w_gate.shape[0] // pieces
    keep = pltpu.make_async_copy(before, out.at[pl.ds(0, height), :], sems.at[2 * pieces])
    loads = []
    for c in range(pieces):
        at = pl.ds(c * size, size)
        for k, (far, here) in enumerate(((w_gate_far, w_gate), (w_up_far, w_up))):
            loads.append(pltpu.make_async_copy(far.at[at, :], here.at[at, :], sems.at[2 * c + k]))
    for load in loads:
        load.start()
    keep.start()
    gate = jnp.zeros((height, w_gate.shape[1]), F32)
    upper = jnp.zeros((height, w_up.shape[1]), F32)
    for c in range(pieces):
        at = slice(c * size, (c + 1) * size)
        loads[2 * c].wait()
        gate = gate + dot(rows[:, at], w_gate[at, :])
        loads[2 * c + 1].wait()
        upper = upper + dot(rows[:, at], w_up[at, :])
    keep.wait()
    out[height:, :] = activate(gate, upper)


def hidden_b(before, rows, w_gate, w_up, pieces=4):
    height, units = before.shape
    inside = pl.BlockSpec(memory_space=pltpu.VMEM)
    outside = pl.BlockSpec(memory_space=pltpu.HBM)
    before, w_gate, w_up = [
        pltpu.with_memory_space_constraint(a, pltpu.HBM) for a in (before, w_gate, w_up)
    ]
    return pl.pallas_call(
        hidden_b_kernel,
        out_shape=jax.ShapeDtypeStruct((2 * height, units), BF16),
        in_specs=[outside, inside, outside, outside],
        out_specs=inside,
        scratch_shapes=[
            pltpu.VMEM(w_gate.shape, BF16),
            pltpu.VMEM(w_up.shape, BF16),
            pltpu.SemaphoreType.DMA((2 * pieces + 1,)),
        ],
        compiler_params=pltpu.CompilerParams(vmem_limit_bytes=16 << 20),
        cost_estimate=pl.CostEstimate(
            flops=4 * height * w_up.size, bytes_accessed=4 * w_up.size, transcendentals=0
        ),
    )(before, rows, w_gate, w_up)


def down_kernel(place, hidden, *refs):
    weights, out = refs[:-1], refs[-1]
    groups, cap, _ = out.shape
    block = weights[0].shape[1]
    count, height, units = hidden.shape
    _, tile, _, own_side = unpack(place)
    for side, weight in enumerate(weights):
        total = jnp.zeros((height, block), F32)
        for k in range(count):
            rows = hidden[lax.bitwise_xor(tile, k)]
            total = total + dot(rows, weight[k * units : (k + 1) * units, :])
        at = pl.multiple_of(lax.bitwise_xor(own_side, side) * block, block)
        total = total.reshape(2, groups, cap // 2, block).astype(BF16)
        for part in range(2):
            slots = slice(part * cap // 2, (part + 1) * cap // 2)
            out[:, slots, pl.ds(at, block)] = total[part]


def combine_kernel(high_a, low_a, high_b, low_b, rows, out):
    count, tok, block = out.shape
    groups, cap, _ = rows.shape
    for k in range(count):
        total = jnp.zeros((tok, block), F32)
        for part, pair in enumerate(((high_a, low_a), (high_b, low_b))):
            slots = slice(part * cap // 2, (part + 1) * cap // 2)
            piece = rows[:, slots, k * block : (k + 1) * block].astype(F32)
            piece = piece.reshape(groups * cap // 2, block).astype(BF16)
            for factor in pair:
                total = total + dot(factor[...], piece, ((0,), (0,)))
        out[k] = total.astype(BF16)


def finish_kernel(parts, out):
    total = parts[0].astype(F32)
    for k in range(1, parts.shape[0]):
        total = total + parts[k].astype(F32)
    out[...] = total.astype(BF16)


def call(kernel, shapes, *args, flops=0, limit=None):
    specs = [pl.BlockSpec(memory_space=pltpu.VMEM)] * len(args)
    if args[0].ndim == 1:
        specs[0] = pl.BlockSpec(memory_space=pltpu.SMEM)
    outs = [jax.ShapeDtypeStruct(s, d) for s, d in shapes]
    moved = sum(a.size * a.dtype.itemsize for a in (*args, *outs))
    return pl.pallas_call(
        kernel,
        out_shape=outs,
        in_specs=specs,
        out_specs=[pl.BlockSpec(memory_space=pltpu.VMEM)] * len(outs),
        compiler_params=pltpu.CompilerParams(vmem_limit_bytes=limit),
        cost_estimate=pl.CostEstimate(flops=flops, bytes_accessed=moved, transcendentals=0),
    )(*args)


def on_device(tokens, routes, probs, w_gate, w_up, w_down):
    groups, shards = lax.axis_size("grp"), lax.axis_size("shard")
    per_group = shards // TPE
    tok, width = tokens.shape
    units = w_down.shape[1]
    block, quarter = width // shards, width // TPE
    cap = 2 * tok * routes.shape[1] // (groups * per_group)
    rows = groups * cap // 2
    room = 16 << 20
    z = lax.axis_index("shard")
    sides = lax.axis_size("side")
    place = (z * TPE + lax.axis_index("side")).astype(jnp.int32).reshape(1)

    def over_y(x):
        return lax.all_to_all(x.reshape(groups, -1, x.shape[-1]), "grp", 0, 0, tiled=True)

    def swap(x, bits, axis="shard"):
        return lax.ppermute(x, axis, [(i, i ^ bits) for i in range(lax.axis_size(axis))])

    factor = ((rows, tok), BF16)

    def dispatch(part, size):
        return call(
            functools.partial(dispatch_kernel, cap, per_group, part),
            [((rows, size), BF16), factor, factor],
            place, routes.T, probs.T, tokens, flops=2 * rows * tok * size,
        )

    sent_a, high_a, low_a = dispatch(0, width // 2)
    mine = over_y(sent_a).reshape(rows, width // 2)
    sent_b, high_b, low_b = dispatch(1, width)
    parts = shuffle(place, w_down[0], block)
    parts = [parts[0]] + [swap(parts[k], k) for k in range(1, TPE)]
    (weight,) = call(stack_kernel, [((units * TPE, block), BF16)], *parts)
    weights = [weight] + [swap(weight, k, "side") for k in range(1, sides)]
    other = swap(mine, 1)
    arrived = over_y(sent_b).reshape(rows, width)
    (hidden,) = call(
        hidden_a_kernel, [((rows, units), BF16)], place, mine, other, w_gate[0], w_up[0],
        flops=4 * rows * width * units,
    )
    hidden = hidden_b(hidden, arrived, w_gate[0], w_up[0])
    quartets = [[i * TPE + k for k in range(TPE)] for i in range(per_group)]
    strided = [[i * TPE + k for i in range(per_group)] for k in range(TPE)]
    hidden = lax.all_gather(hidden, "shard", axis_index_groups=quartets)
    weights = [pltpu.with_memory_space_constraint(w, pltpu.VMEM) for w in weights]
    (result,) = call(
        down_kernel, [((groups, cap, quarter), BF16)], place, hidden, *weights,
        flops=4 * rows * width * units, limit=room,
    )
    returned = over_y(result)
    (parts,) = call(
        combine_kernel, [((per_group, tok, block), BF16)],
        high_a, low_a, high_b, low_b, returned, limit=room,
    )
    parts = lax.all_to_all(parts, "shard", 0, 0, tiled=True, axis_index_groups=strided)
    (mixed,) = call(finish_kernel, [((tok, block), BF16)], parts, limit=room)
    return mixed


def solution(mesh):
    return jax.shard_map(
        on_device,
        mesh=mesh,
        in_specs=(
            P(("grp", "side"), None),
            P(("grp", "side"), None),
            P(("grp", "side"), None),
            P(("grp", "shard"), None, None),
            P(("grp", "shard"), None, None),
            P(("grp", "shard"), None, None),
        ),
        out_specs=P(("grp", "side"), "shard"),
        check_vma=False,
    )
```

```python
import functools

import jax
import jax.numpy as jnp
from jax import lax
from jax.experimental import pallas as pl
from jax.experimental.pallas import tpu as pltpu
from jax.sharding import PartitionSpec as P


TPE = 4
BF16 = jnp.bfloat16
F32 = jnp.float32


def dot(a, b, dims=((1,), (0,))):
    return lax.dot_general(a, b, (dims, ((), ())), preferred_element_type=F32)


def unpack(place):
    z = lax.shift_right_logical(place[0], 2)
    quartet, tile = lax.shift_right_logical(z, 2), lax.bitwise_and(z, 3)
    return quartet, tile, lax.bitwise_and(z, 1), lax.bitwise_and(place[0], 3)


def dispatch_kernel(cap, per_group, part, place, routes, tokens, sent):
    tok = tokens.shape[0]
    rows, width = sent.shape
    half = cap // 2
    before = lax.broadcasted_iota(jnp.int32, (tok, tok), 0)
    before = before < lax.broadcasted_iota(jnp.int32, (tok, tok), 1)
    before = jnp.where(before, F32(1.0), F32(0.0)).astype(BF16)
    row = lax.broadcasted_iota(jnp.int32, (rows, tok), 0)
    target = lax.shift_right_logical(row, half.bit_length() - 1) * per_group + unpack(place)[0]
    slot = (lax.bitwise_and(row, half - 1) + part * half).astype(F32)
    hits = jnp.zeros((rows, tok), F32)
    for k in range(routes.shape[0]):
        hits = jnp.where(routes[k : k + 1, :] == target, F32(1.0), hits)
    ranks = dot(hits.astype(BF16), before)
    chosen = (hits > 0.5) & (ranks == slot)
    select = jnp.where(chosen, F32(1.0), F32(0.0)).astype(BF16)
    step = min(512, width)
    for at in range(0, width, step):
        start = unpack(place)[2] * width + at if part == 0 else at
        piece = tokens[:, pl.ds(pl.multiple_of(start, step), step)]
        sent[:, at : at + step] = dot(select, piece).astype(BF16)


def factor_kernel(cap, routes, probs, high, low):
    rows, tok = high.shape
    gates = probs[...] / jnp.sum(probs[...], axis=0, keepdims=True)
    before = lax.broadcasted_iota(jnp.int32, (tok, tok), 0)
    before = before < lax.broadcasted_iota(jnp.int32, (tok, tok), 1)
    before = jnp.where(before, F32(1.0), F32(0.0)).astype(BF16)
    row = lax.broadcasted_iota(jnp.int32, (rows, tok), 0)
    target = lax.shift_right_logical(row, cap.bit_length() - 1)
    slot = lax.bitwise_and(row, cap - 1).astype(F32)
    hits = jnp.zeros((rows, tok), F32)
    weight = jnp.zeros((rows, tok), F32)
    for k in range(routes.shape[0]):
        match = routes[k : k + 1, :] == target
        hits = jnp.where(match, F32(1.0), hits)
        weight = jnp.where(match, gates[k : k + 1, :], weight)
    chosen = (hits > 0.5) & (dot(hits.astype(BF16), before) == slot)
    weight = jnp.where(chosen, weight, F32(0.0))
    top = weight.astype(BF16)
    high[...] = top
    low[...] = (weight - top.astype(F32)).astype(BF16)


def shuffle_kernel(place, weights, *refs):
    outs, sems = refs[:-1], refs[-1]
    _, tile, _, side = unpack(place)
    block = outs[0].shape[1]
    loads = []
    for k, out in enumerate(outs):
        at = pl.multiple_of((side * TPE + lax.bitwise_xor(tile, k)) * block, block)
        loads.append(pltpu.make_async_copy(weights.at[:, pl.ds(at, block)], out, sems.at[k]))
    for load in loads:
        load.start()
    for load in loads:
        load.wait()


def shuffle(place, weights, block):
    return pl.pallas_call(
        shuffle_kernel,
        out_shape=[jax.ShapeDtypeStruct((weights.shape[0], block), BF16)] * TPE,
        in_specs=[pl.BlockSpec(memory_space=pltpu.SMEM), pl.BlockSpec(memory_space=pltpu.HBM)],
        out_specs=[pl.BlockSpec(memory_space=pltpu.VMEM)] * TPE,
        scratch_shapes=[pltpu.SemaphoreType.DMA((TPE,))],
        compiler_params=pltpu.CompilerParams(vmem_limit_bytes=16 << 20),
        cost_estimate=pl.CostEstimate(
            flops=0, bytes_accessed=4 * TPE * weights.shape[0] * block, transcendentals=0
        ),
    )(place, pltpu.with_memory_space_constraint(weights, pltpu.HBM))


def stack_kernel(*refs):
    size = refs[0].shape[0]
    for k, ref in enumerate(refs[:-1]):
        refs[-1][k * size : (k + 1) * size, :] = ref[...]


def activate(gate, upper):
    return (gate / (1.0 + jnp.exp(-gate)) * upper).astype(BF16)


def hidden_a_kernel(place, mine, other, w_gate, w_up, out):
    width = mine.shape[1]
    parity = unpack(place)[2]
    own = pl.ds(pl.multiple_of(parity * width, width), width)
    far = pl.ds(pl.multiple_of((1 - parity) * width, width), width)
    gate = dot(mine[...], w_gate[own, :]) + dot(other[...], w_gate[far, :])
    upper = dot(mine[...], w_up[own, :]) + dot(other[...], w_up[far, :])
    out[...] = activate(gate, upper)


def hidden_b_kernel(before, rows, w_gate_far, w_up_far, out, w_gate, w_up, sems):
    height, pieces = before.shape[0], sems.shape[0] // 2
    size = w_gate.shape[0] // pieces
    keep = pltpu.make_async_copy(before, out.at[pl.ds(0, height), :], sems.at[2 * pieces])
    loads = []
    for c in range(pieces):
        at = pl.ds(c * size, size)
        for k, (far, here) in enumerate(((w_gate_far, w_gate), (w_up_far, w_up))):
            loads.append(pltpu.make_async_copy(far.at[at, :], here.at[at, :], sems.at[2 * c + k]))
    for load in loads:
        load.start()
    keep.start()
    gate = jnp.zeros((height, w_gate.shape[1]), F32)
    upper = jnp.zeros((height, w_up.shape[1]), F32)
    for c in range(pieces):
        at = slice(c * size, (c + 1) * size)
        loads[2 * c].wait()
        gate = gate + dot(rows[:, at], w_gate[at, :])
        loads[2 * c + 1].wait()
        upper = upper + dot(rows[:, at], w_up[at, :])
    keep.wait()
    out[height:, :] = activate(gate, upper)


def hidden_b(before, rows, w_gate, w_up, pieces=4):
    height, units = before.shape
    inside = pl.BlockSpec(memory_space=pltpu.VMEM)
    outside = pl.BlockSpec(memory_space=pltpu.HBM)
    before, w_gate, w_up = [
        pltpu.with_memory_space_constraint(a, pltpu.HBM) for a in (before, w_gate, w_up)
    ]
    return pl.pallas_call(
        hidden_b_kernel,
        out_shape=jax.ShapeDtypeStruct((2 * height, units), BF16),
        in_specs=[outside, inside, outside, outside],
        out_specs=inside,
        scratch_shapes=[
            pltpu.VMEM(w_gate.shape, BF16),
            pltpu.VMEM(w_up.shape, BF16),
            pltpu.SemaphoreType.DMA((2 * pieces + 1,)),
        ],
        compiler_params=pltpu.CompilerParams(vmem_limit_bytes=16 << 20),
        cost_estimate=pl.CostEstimate(
            flops=4 * height * w_up.size, bytes_accessed=4 * w_up.size, transcendentals=0
        ),
    )(before, rows, w_gate, w_up)


def down_kernel(place, hidden, *refs):
    weights, out = refs[:-1], refs[-1]
    groups, _, cap, block = out.shape
    count, height, units = hidden.shape
    _, tile, _, own_side = unpack(place)
    for side, weight in enumerate(weights):
        total = jnp.zeros((height, block), F32)
        for k in range(count):
            rows = hidden[lax.bitwise_xor(tile, k)]
            total = total + dot(rows, weight[k * units : (k + 1) * units, :])
        at = lax.bitwise_xor(own_side, side)
        total = total.reshape(2, groups, cap // 2, block).astype(BF16)
        for part in range(2):
            slots = slice(part * cap // 2, (part + 1) * cap // 2)
            out[:, at, slots, :] = total[part]


def combine_kernel(high, low, rows, out):
    total = dot(high[...], rows[...], ((0,), (0,))) + dot(low[...], rows[...], ((0,), (0,)))
    out[...] = total.astype(BF16)


def call(kernel, shapes, *args, flops=0, limit=None):
    specs = [pl.BlockSpec(memory_space=pltpu.VMEM)] * len(args)
    if args[0].ndim == 1:
        specs[0] = pl.BlockSpec(memory_space=pltpu.SMEM)
    outs = [jax.ShapeDtypeStruct(s, d) for s, d in shapes]
    moved = sum(a.size * a.dtype.itemsize for a in (*args, *outs))
    return pl.pallas_call(
        kernel,
        out_shape=outs,
        in_specs=specs,
        out_specs=[pl.BlockSpec(memory_space=pltpu.VMEM)] * len(outs),
        compiler_params=pltpu.CompilerParams(vmem_limit_bytes=limit),
        cost_estimate=pl.CostEstimate(flops=flops, bytes_accessed=moved, transcendentals=0),
    )(*args)


def on_device(tokens, routes, probs, w_gate, w_up, w_down):
    groups, shards = lax.axis_size("grp"), lax.axis_size("shard")
    per_group = shards // TPE
    tok, width = tokens.shape
    units = w_down.shape[1]
    block = width // shards
    cap = 2 * tok * routes.shape[1] // (groups * per_group)
    rows = groups * cap // 2
    room = 16 << 20
    z = lax.axis_index("shard")
    sides = lax.axis_size("side")
    place = (z * TPE + lax.axis_index("side")).astype(jnp.int32).reshape(1)

    def over_y(x):
        return lax.all_to_all(x.reshape(groups, -1, x.shape[-1]), "grp", 0, 0, tiled=True)

    def swap(x, bits, axis="shard"):
        return lax.ppermute(x, axis, [(i, i ^ bits) for i in range(lax.axis_size(axis))])

    def dispatch(part, size):
        (sent,) = call(
            functools.partial(dispatch_kernel, cap, per_group, part),
            [((rows, size), BF16)],
            place, routes.T, tokens, flops=2 * rows * tok * size,
        )
        return sent

    sent_a = dispatch(0, width // 2)
    mine = over_y(sent_a).reshape(rows, width // 2)
    sent_b = dispatch(1, width)
    slots = groups * per_group * cap
    high, low = call(
        functools.partial(factor_kernel, cap), [((slots, tok), BF16)] * 2,
        routes.T, probs.T, flops=2 * slots * tok * tok,
    )
    parts = shuffle(place, w_down[0], block)
    parts = [parts[0]] + [swap(parts[k], k) for k in range(1, TPE)]
    (weight,) = call(stack_kernel, [((units * TPE, block), BF16)], *parts)
    weights = [weight] + [swap(weight, k, "side") for k in range(1, sides)]
    other = swap(mine, 1)
    arrived = over_y(sent_b).reshape(rows, width)
    (hidden,) = call(
        hidden_a_kernel, [((rows, units), BF16)], place, mine, other, w_gate[0], w_up[0],
        flops=4 * rows * width * units,
    )
    hidden = hidden_b(hidden, arrived, w_gate[0], w_up[0])
    quartets = [[i * TPE + k for k in range(TPE)] for i in range(per_group)]
    hidden = lax.all_gather(hidden, "shard", axis_index_groups=quartets)
    weights = [pltpu.with_memory_space_constraint(w, pltpu.VMEM) for w in weights]
    (result,) = call(
        down_kernel, [((groups, TPE, cap, block), BF16)], place, hidden, *weights,
        flops=4 * rows * width * units, limit=room,
    )
    homes = [
        [(g * per_group + q) * TPE + k for g in range(groups) for q in range(per_group)]
        for k in range(TPE)
    ]
    result = result.reshape(groups * TPE, cap, block)
    returned = lax.all_to_all(
        result, ("grp", "shard"), 0, 0, tiled=True, axis_index_groups=homes
    ).reshape(slots, block)
    (mixed,) = call(
        combine_kernel, [((tok, block), BF16)], high, low, returned,
        flops=4 * slots * tok * block, limit=room,
    )
    return mixed


def solution(mesh):
    return jax.shard_map(
        on_device,
        mesh=mesh,
        in_specs=(
            P(("grp", "side"), None),
            P(("grp", "side"), None),
            P(("grp", "side"), None),
            P(("grp", "shard"), None, None),
            P(("grp", "shard"), None, None),
            P(("grp", "shard"), None, None),
        ),
        out_specs=P(("grp", "side"), "shard"),
        check_vma=False,
    )
```
